8 devices in a mesh: dp: 2 (over z, y), fsdp: 4 (over x, core).
Axes of the slice: x: 2, y: 2, z: 1, core: 2. Of those that a mesh axis runs over, the one named last changes fastest.
Arguments:
- u_in: bfloat16 [8, 1024, 2560], P(('dp', 'fsdp'))
- grad_out: bfloat16 [8, 1024, 2560], P(('dp', 'fsdp'))
- norm_w: bfloat16 [2, 2560], P(None, 'fsdp')
- w_in: bfloat16 [2, 2560, 10576], P(None, 'fsdp')
- conv_w: bfloat16 [2, 4, 5376], P(None, None, 'fsdp')
- conv_b: bfloat16 [2, 5376], P(None, 'fsdp')
- dt_bias: float32 [2, 80], P(None, 'fsdp')
- a_log: float32 [2, 80], P(None, 'fsdp')
- d_skip: float32 [2, 80], P(None, 'fsdp')
- gate_w: bfloat16 [2, 5120], P(None, 'fsdp')
- w_out: bfloat16 [2, 5120, 2560], P(None, 'fsdp')
Outputs:
- output 1: bfloat16 [8, 1024, 2560], P(('dp', 'fsdp'))
- output 2: bfloat16 [8, 1024, 2560], P(('dp', 'fsdp'))
- output 3: float32 [2, 2560], P(None, 'fsdp')
- output 4: float32 [2, 2560, 10576], P(None, 'fsdp')
- output 5: float32 [2, 4, 5376], P(None, None, 'fsdp')
- output 6: float32 [2, 5376], P(None, 'fsdp')
- output 7: float32 [2, 80], P(None, 'fsdp')
- output 8: float32 [2, 80], P(None, 'fsdp')
- output 9: float32 [2, 80], P(None, 'fsdp')
- output 10: float32 [2, 5120], P(None, 'fsdp')
- output 11: float32 [2, 5120, 2560], P(None, 'fsdp')
All inputs are finite; a program needn't handle non-finite values.
Results may differ from the reference program's by a relative error of at most 0.02.
Values are sent between devices in bfloat16 or wider.
A program may use at most 1 GiB of HBM per device.

```python
import jax
import jax.numpy as jnp
from jax import lax

D_MODEL = 2560
D_INNER = 5120
N_HEADS = 80
HEAD_DIM = 64
D_STATE = 128
N_GROUPS = 1
CONV_WIDTH = 4
CHUNK_LEN = 256
SEQ_LEN = 1024
BATCH_TOT = 8
CONV_DIM = D_INNER + 2 * N_GROUPS * D_STATE
PROJ_DIM = 2 * D_INNER + 2 * N_GROUPS * D_STATE + N_HEADS
PER_GROUP = N_HEADS // N_GROUPS
NORM_EPS = 1e-5


def setup_inputs(seed: int = 0) -> dict:
    keys = jax.random.split(jax.random.key(seed), 11)

    def normal(key_i, shape, scale):
        return jax.random.normal(key_i, shape, jnp.float32) * scale

    act_shape = (BATCH_TOT, SEQ_LEN, D_MODEL)
    return {
        'u_in': normal(keys[0], act_shape, 1.0).astype(jnp.bfloat16),
        'grad_out': normal(keys[1], act_shape, 1.0).astype(jnp.bfloat16),
        'norm_w': (1.0 + normal(keys[2], (2, D_MODEL), 0.3)).astype(jnp.bfloat16),
        'w_in': normal(keys[3], (2, D_MODEL, PROJ_DIM), D_MODEL ** -0.5).astype(jnp.bfloat16),
        'conv_w': normal(keys[4], (2, CONV_WIDTH, CONV_DIM), CONV_WIDTH ** -0.5).astype(jnp.bfloat16),
        'conv_b': normal(keys[5], (2, CONV_DIM), 0.5).astype(jnp.bfloat16),
        'dt_bias': normal(keys[6], (2, N_HEADS), 1.0) - 2.0,
        'a_log': jnp.log(jax.random.uniform(keys[7], (2, N_HEADS), jnp.float32, 1.0, 16.0)),
        'd_skip': 1.0 + normal(keys[8], (2, N_HEADS), 0.5),
        'gate_w': (1.0 + normal(keys[9], (2, D_INNER), 0.3)).astype(jnp.bfloat16),
        'w_out': normal(keys[10], (2, D_INNER, D_MODEL), D_INNER ** -0.5).astype(jnp.bfloat16),
    }


def pre_norm(u_rows, norm_w):
    rows_f = u_rows.astype(jnp.float32)
    inv_rms = lax.rsqrt(jnp.mean(rows_f * rows_f, axis=-1, keepdims=True) + NORM_EPS)
    return (rows_f * inv_rms * norm_w.astype(jnp.float32)).astype(jnp.bfloat16)


def ssd_chunks(x_heads, dt_heads, a_heads, b_mat, c_mat):
    n_chunks = x_heads.shape[0] // CHUNK_LEN
    x_dt = (x_heads * dt_heads[:, :, None]).reshape(n_chunks, CHUNK_LEN, N_GROUPS, PER_GROUP, HEAD_DIM)
    cum_a = jnp.cumsum(a_heads.reshape(n_chunks, CHUNK_LEN, N_GROUPS, PER_GROUP), axis=1)
    b_chunk = b_mat.reshape(n_chunks, CHUNK_LEN, N_GROUPS, D_STATE).astype(jnp.float32)
    c_chunk = c_mat.reshape(n_chunks, CHUNK_LEN, N_GROUPS, D_STATE).astype(jnp.float32)
    scores = jnp.einsum('cqgn,csgn->cgqs', c_chunk, b_chunk)
    cum_t = jnp.moveaxis(cum_a, 1, -1)
    log_gap = cum_t[..., :, None] - cum_t[..., None, :]
    causal = jnp.arange(CHUNK_LEN)[:, None] >= jnp.arange(CHUNK_LEN)[None, :]
    decay_mat = jnp.where(causal, jnp.exp(jnp.where(causal, log_gap, 0.0)), 0.0)
    y_diag = jnp.einsum('cgrqs,csgrp->cqgrp', scores[:, :, None] * decay_mat, x_dt)
    end_decay = jnp.exp(cum_a[:, -1:] - cum_a)
    states = jnp.einsum('csgn,csgrp->cgrpn', b_chunk, x_dt * end_decay[..., None])
    totals = cum_a[:, -1]
    incl_sum = jnp.cumsum(totals, axis=0)
    excl_sum = incl_sum - totals
    chunk_gap = jnp.moveaxis(excl_sum, 0, -1)[..., :, None] - jnp.moveaxis(incl_sum, 0, -1)[..., None, :]
    earlier = jnp.arange(n_chunks)[:, None] > jnp.arange(n_chunks)[None, :]
    carry_mat = jnp.where(earlier, jnp.exp(jnp.where(earlier, chunk_gap, 0.0)), 0.0)
    prev_state = jnp.einsum('grij,jgrpn->igrpn', carry_mat, states)
    y_off = jnp.einsum('cqgn,cgrpn->cqgrp', c_chunk, prev_state) * jnp.exp(cum_a)[..., None]
    return (y_diag + y_off).reshape(x_heads.shape)


def mamba_layer(u_seq, layer_w):
    norm_w, w_in, conv_w, conv_b, dt_bias, a_log, d_skip, gate_w, w_out = layer_w
    seq_len = u_seq.shape[0]
    h_norm = pre_norm(u_seq, norm_w)
    proj_out = jnp.dot(h_norm, w_in, preferred_element_type=jnp.float32).astype(jnp.bfloat16)
    xbc = proj_out[:, D_INNER:D_INNER + CONV_DIM].astype(jnp.float32)
    padded = jnp.pad(xbc, ((CONV_WIDTH - 1, 0), (0, 0)))
    conv_out = conv_b.astype(jnp.float32) + sum(padded[tap:tap + seq_len] * conv_w[tap].astype(jnp.float32) for tap in range(CONV_WIDTH))
    xbc_act = jax.nn.silu(conv_out)
    group_w = N_GROUPS * D_STATE
    x_heads = xbc_act[:, :D_INNER].reshape(seq_len, N_HEADS, HEAD_DIM)
    b_mat = xbc_act[:, D_INNER:D_INNER + group_w].reshape(seq_len, N_GROUPS, D_STATE)
    c_mat = xbc_act[:, D_INNER + group_w:].reshape(seq_len, N_GROUPS, D_STATE)
    dt_heads = jax.nn.softplus(proj_out[:, D_INNER + CONV_DIM:].astype(jnp.float32) + dt_bias)
    a_heads = dt_heads * -jnp.exp(a_log)
    y_heads = ssd_chunks(x_heads, dt_heads, a_heads, b_mat, c_mat) + d_skip[:, None] * x_heads
    z_act = jax.nn.silu(proj_out[:, :D_INNER].astype(jnp.float32))
    gated_y = y_heads.reshape(seq_len, N_GROUPS, -1) * z_act.reshape(seq_len, N_GROUPS, -1)
    normed = gated_y * lax.rsqrt(jnp.mean(gated_y * gated_y, axis=-1, keepdims=True) + NORM_EPS)
    y_norm = (normed.reshape(seq_len, D_INNER) * gate_w.astype(jnp.float32)).astype(jnp.bfloat16)
    mixed = jnp.dot(y_norm, w_out, preferred_element_type=jnp.float32)
    return (u_seq.astype(jnp.float32) + mixed).astype(jnp.bfloat16)


def reference(u_in, grad_out, norm_w, w_in, conv_w, conv_b, dt_bias, a_log, d_skip, gate_w, w_out):
    params = (norm_w, w_in, conv_w, conv_b, dt_bias, a_log, d_skip, gate_w, w_out)

    def two_layers(u_seq, stack_w):
        hidden = mamba_layer(u_seq, [w_l[0] for w_l in stack_w])
        return mamba_layer(hidden, [w_l[1] for w_l in stack_w])

    def per_sequence(acc, pair):
        u_seq, g_seq = pair
        out_seq, pull = jax.vjp(two_layers, u_seq, params)
        du_seq, d_params = pull(g_seq)
        acc = tuple(total + grad_w.astype(jnp.float32) for total, grad_w in zip(acc, d_params))
        return acc, (out_seq, du_seq)

    zeros = tuple(jnp.zeros(w_l.shape, jnp.float32) for w_l in params)
    sums, (out, d_u) = lax.scan(per_sequence, zeros, (u_in, grad_out))
    return (out, d_u) + tuple(total / BATCH_TOT for total in sums)
```

```python
import functools

import jax
import jax.numpy as jnp
from jax import lax
from jax.experimental import pallas as pl
from jax.experimental.layout import Layout, with_layout_constraint
from jax.experimental.pallas import tpu as pltpu
from jax.sharding import PartitionSpec as P

CHUNK_LEN = 256
STATE_DIM = 128
HEAD_DIM = 64
HEADS_BLK = 8
LANES_BLK = HEADS_BLK * HEAD_DIM
NORM_EPS = 1e-5
F32 = jnp.float32
BF16 = jnp.bfloat16


def row_major(arr):
    return with_layout_constraint(arr, Layout(major_to_minor=tuple(range(arr.ndim))))


def dot_nn(a, b):
    return lax.dot_general(a, b, (((1,), (0,)), ((), ())), preferred_element_type=F32)


def dot_nt(a, b):
    return lax.dot_general(a, b, (((1,), (1,)), ((), ())), preferred_element_type=F32)


def dot_tn(a, b):
    return lax.dot_general(a, b, (((0,), (0,)), ((), ())), preferred_element_type=F32)


def spread_heads(cols, lane):
    rows = cols.shape[0]
    parts = []
    for pair in range(HEADS_BLK // 2):
        left = jnp.broadcast_to(cols[:, 2 * pair:2 * pair + 1], (rows, 128))
        right = jnp.broadcast_to(cols[:, 2 * pair + 1:2 * pair + 2], (rows, 128))
        parts.append(jnp.where(lane[:rows] < HEAD_DIM, left, right))
    return jnp.concatenate(parts, axis=1)


def head_sums(vals, seg):
    hi = vals.astype(BF16)
    rest = vals - hi.astype(F32)
    mid = rest.astype(BF16)
    low = (rest - mid.astype(F32)).astype(BF16)
    return dot_nn(hi, seg) + dot_nn(mid, seg) + dot_nn(low, seg)


def ssd_fwd_kernel(x_ref, b_ref, c_ref, dt_ref, cum_ref, cumt_ref, skip_ref, y_ref, prev_ref, state, scores):
    chunk = pl.program_id(0)
    blk = pl.program_id(1)
    b_mat = b_ref[...].astype(BF16)
    c_mat = c_ref[...].astype(BF16)

    @pl.when(chunk == 0)
    def _():
        state[blk] = jnp.zeros((STATE_DIM, LANES_BLK), F32)

    @pl.when(blk == 0)
    def _():
        scores[...] = dot_nt(c_mat, b_mat)

    lane = lax.broadcasted_iota(jnp.int32, (CHUNK_LEN, 128), 1)
    causal = lax.broadcasted_iota(jnp.int32, (CHUNK_LEN, CHUNK_LEN), 0) >= lax.broadcasted_iota(jnp.int32, (CHUNK_LEN, CHUNK_LEN), 1)
    x_blk = x_ref[...]
    cum = cum_ref[0]
    cum_e = spread_heads(cum, lane)
    tot_e = cum_e[CHUNK_LEN - 1:CHUNK_LEN, :]
    x_dt = x_blk * spread_heads(dt_ref[0], lane)
    xd_b = x_dt.astype(BF16)
    prev = state[blk]
    prev_ref[0] = prev
    y_off = dot_nn(c_mat, prev.astype(BF16)) * jnp.exp(cum_e)
    state[blk] = prev * jnp.exp(tot_e) + dot_tn(b_mat, (x_dt * jnp.exp(tot_e - cum_e)).astype(BF16))
    g_mat = scores[...]
    zero = jnp.zeros((CHUNK_LEN, 128), BF16)
    for pair in range(HEADS_BLK // 2):
        cols = slice(pair * 128, pair * 128 + 128)
        acc = y_off[:, cols] + skip_ref[:, cols] * x_blk[:, cols]
        for side in range(2):
            head = 2 * pair + side
            gap = cum[:, head:head + 1] - cumt_ref[0][head:head + 1, :]
            decay = jnp.exp(jnp.where(causal, gap, -1e30))
            mine = (lane < HEAD_DIM) if side == 0 else (lane >= HEAD_DIM)
            acc = acc + dot_nn((g_mat * decay).astype(BF16), jnp.where(mine, xd_b[:, cols], zero))
        y_ref[:, cols] = acc


def ssd_bwd_kernel(dy_ref, y_ref, x_ref, b_ref, c_ref, dt_ref, cum_ref, cumt_ref, skip_ref, prev_ref,
                   dxbc_ref, dcum_ref, ddt_ref, dskip_ref, d_state, scores_t, dg_t, d_b, d_c, *, n_blk):
    rev = pl.program_id(0)
    blk = pl.program_id(1)
    b_mat = b_ref[...].astype(BF16)
    c_mat = c_ref[...].astype(BF16)

    @pl.when(blk == 0)
    def _():
        scores_t[...] = dot_nt(b_mat, c_mat)
        dg_t[...] = jnp.zeros_like(dg_t)
        d_b[...] = jnp.zeros_like(d_b)
        d_c[...] = jnp.zeros_like(d_c)

    @pl.when((rev == 0) & (blk < n_blk))
    def _():
        d_state[blk] = jnp.zeros((STATE_DIM, LANES_BLK), F32)

    @pl.when(blk < n_blk)
    def _():
        lane = lax.broadcasted_iota(jnp.int32, (CHUNK_LEN, 128), 1)
        row = lax.broadcasted_iota(jnp.int32, (CHUNK_LEN, 128), 0)
        causal = lax.broadcasted_iota(jnp.int32, (CHUNK_LEN, CHUNK_LEN), 0) <= lax.broadcasted_iota(jnp.int32, (CHUNK_LEN, CHUNK_LEN), 1)
        seg = (lax.broadcasted_iota(jnp.int32, (LANES_BLK, 128), 0) // HEAD_DIM == lax.broadcasted_iota(jnp.int32, (LANES_BLK, 128), 1))
        seg = jnp.where(seg, 1.0, 0.0).astype(BF16)
        x_blk = x_ref[...]
        dy = dy_ref[...]
        cum = cum_ref[0]
        cum_e = spread_heads(cum, lane)
        tot_e = cum_e[CHUNK_LEN - 1:CHUNK_LEN, :]
        dt_e = spread_heads(dt_ref[0], lane)
        x_dt = x_blk * dt_e
        xd_b = x_dt.astype(BF16)
        dy_b = dy.astype(BF16)
        skip = skip_ref[...]
        prev = prev_ref[0]
        prev_b = prev.astype(BF16)
        d_next = d_state[blk]
        dn_b = d_next.astype(BF16)
        end_decay = jnp.exp(tot_e - cum_e)
        dy_in = (dy * jnp.exp(cum_e)).astype(BF16)
        tail = dot_nn(b_mat, dn_b) * end_decay
        d_b[...] += dot_nt((x_dt * end_decay).astype(BF16), dn_b)
        d_c[...] += dot_nt(dy_in, prev_b)
        d_state[blk] = d_next * jnp.exp(tot_e) + dot_tn(c_mat, dy_in)
        r_in = x_dt * tail
        tot_grad = jnp.sum(r_in, axis=0, keepdims=True) + jnp.exp(tot_e) * jnp.sum(prev * d_next, axis=0, keepdims=True)
        g_t = scores_t[...]
        zero = jnp.zeros((CHUNK_LEN, 128), BF16)
        dg_sum = None
        diag_parts = []
        for pair in range(HEADS_BLK // 2):
            cols = slice(pair * 128, pair * 128 + 128)
            acc = None
            for side in range(2):
                head = 2 * pair + side
                gap = cumt_ref[0][head:head + 1, :] - cum[:, head:head + 1]
                decay = jnp.exp(jnp.where(causal, gap, -1e30))
                mine = (lane < HEAD_DIM) if side == 0 else (lane >= HEAD_DIM)
                dy_m = jnp.where(mine, dy_b[:, cols], zero)
                part = dot_nn((g_t * decay).astype(BF16), dy_m)
                acc = part if acc is None else acc + part
                dg = dot_nt(xd_b[:, cols], dy_m) * decay
                dg_sum = dg if dg_sum is None else dg_sum + dg
            diag_parts.append(acc)
        dg_t[...] += dg_sum
        diag = jnp.concatenate(diag_parts, axis=1)
        d_xdt = diag + tail
        y_ssd = y_ref[...] - skip * x_blk
        dxbc_ref[...] = d_xdt * dt_e + skip * dy
        ddt_ref[...] = head_sums(d_xdt * x_blk, seg)
        flow = dy_b.astype(F32) * y_ssd - xd_b.astype(F32) * diag - r_in
        last = lax.broadcasted_iota(jnp.int32, (CHUNK_LEN, LANES_BLK), 0) == CHUNK_LEN - 1
        flow = flow + jnp.where(last, jnp.broadcast_to(tot_grad, flow.shape), 0.0)
        dcum_ref[...] = head_sums(flow, seg)
        dskip_ref[0] = jnp.sum((dy * x_blk).reshape(CHUNK_LEN // 8, 8, LANES_BLK), axis=0)

    @pl.when(blk == n_blk)
    def _():
        dg_b = dg_t[...].astype(BF16)
        dxbc_ref[:, :STATE_DIM] = d_b[...] + dot_nn(dg_b, c_mat)
        dxbc_ref[:, STATE_DIM:2 * STATE_DIM] = d_c[...] + dot_tn(dg_b, b_mat)
        dxbc_ref[:, 2 * STATE_DIM:] = jnp.zeros((CHUNK_LEN, LANES_BLK - 2 * STATE_DIM), F32)


def head_tables(dt_heads, a_heads):
    seq_len, n_heads = dt_heads.shape
    n_chunks = seq_len // CHUNK_LEN
    lower = jnp.tril(jnp.ones((CHUNK_LEN, CHUNK_LEN), F32))
    cum = jnp.einsum('qs,csh->cqh', lower, a_heads.reshape(n_chunks, CHUNK_LEN, n_heads), precision=lax.Precision.HIGHEST)
    cum = cum.reshape(seq_len, n_heads // HEADS_BLK, HEADS_BLK)
    dt_blk = dt_heads.reshape(seq_len, n_heads // HEADS_BLK, HEADS_BLK).transpose(1, 0, 2)
    return dt_blk, cum.transpose(1, 0, 2), cum.transpose(1, 2, 0)


def ssd_forward(xbc_act, dt_blk, cum_blk, cum_t, skip_row):
    seq_len = xbc_act.shape[0]
    n_blk = dt_blk.shape[0]
    d_inner = n_blk * LANES_BLK
    n_chunks = seq_len // CHUNK_LEN
    b_col = d_inner // STATE_DIM
    return pl.pallas_call(
        ssd_fwd_kernel,
        grid=(n_chunks, n_blk),
        in_specs=[
            pl.BlockSpec((CHUNK_LEN, LANES_BLK), lambda c, h: (c, h)),
            pl.BlockSpec((CHUNK_LEN, STATE_DIM), lambda c, h: (c, b_col)),
            pl.BlockSpec((CHUNK_LEN, STATE_DIM), lambda c, h: (c, b_col + 1)),
            pl.BlockSpec((1, CHUNK_LEN, HEADS_BLK), lambda c, h: (h, c, 0)),
            pl.BlockSpec((1, CHUNK_LEN, HEADS_BLK), lambda c, h: (h, c, 0)),
            pl.BlockSpec((1, HEADS_BLK, CHUNK_LEN), lambda c, h: (h, 0, c)),
            pl.BlockSpec((1, LANES_BLK), lambda c, h: (0, h)),
        ],
        out_specs=[
            pl.BlockSpec((CHUNK_LEN, LANES_BLK), lambda c, h: (c, h)),
            pl.BlockSpec((1, STATE_DIM, LANES_BLK), lambda c, h: (c, 0, h)),
        ],
        out_shape=[
            jax.ShapeDtypeStruct((seq_len, d_inner), F32),
            jax.ShapeDtypeStruct((n_chunks, STATE_DIM, d_inner), F32),
        ],
        scratch_shapes=[
            pltpu.VMEM((n_blk, STATE_DIM, LANES_BLK), F32),
            pltpu.VMEM((CHUNK_LEN, CHUNK_LEN), F32),
        ],
        compiler_params=pltpu.CompilerParams(dimension_semantics=('arbitrary', 'arbitrary'), vmem_limit_bytes=40 * 2**20),
        cost_estimate=pl.CostEstimate(flops=60_000_000_000, bytes_accessed=50_000_000, transcendentals=0),
        name='ssd_forward',
    )(xbc_act, xbc_act, xbc_act, dt_blk, cum_blk, cum_t, skip_row)


def ssd_backward(dy, y_all, xbc_act, dt_blk, cum_blk, cum_t, skip_row, prev_states):
    seq_len, conv_dim = xbc_act.shape
    n_blk = dt_blk.shape[0]
    d_inner = n_blk * LANES_BLK
    n_chunks = seq_len // CHUNK_LEN
    b_col = d_inner // STATE_DIM
    top = n_chunks - 1
    cap = n_blk - 1
    wide = pl.BlockSpec((CHUNK_LEN, LANES_BLK), lambda c, h: (top - c, jnp.minimum(h, cap)))
    table = pl.BlockSpec((1, CHUNK_LEN, HEADS_BLK), lambda c, h: (jnp.minimum(h, cap), top - c, 0))
    sums = pl.BlockSpec((CHUNK_LEN, 128), lambda c, h: (top - c, jnp.minimum(h, cap)))
    return pl.pallas_call(
        functools.partial(ssd_bwd_kernel, n_blk=n_blk),
        grid=(n_chunks, n_blk + 1),
        in_specs=[
            wide, wide, wide,
            pl.BlockSpec((CHUNK_LEN, STATE_DIM), lambda c, h: (top - c, b_col)),
            pl.BlockSpec((CHUNK_LEN, STATE_DIM), lambda c, h: (top - c, b_col + 1)),
            table, table,
            pl.BlockSpec((1, HEADS_BLK, CHUNK_LEN), lambda c, h: (jnp.minimum(h, cap), 0, top - c)),
            pl.BlockSpec((1, LANES_BLK), lambda c, h: (0, jnp.minimum(h, cap))),
            pl.BlockSpec((1, STATE_DIM, LANES_BLK), lambda c, h: (top - c, 0, jnp.minimum(h, cap))),
        ],
        out_specs=[
            pl.BlockSpec((CHUNK_LEN, LANES_BLK), lambda c, h: (top - c, h)),
            sums, sums,
            pl.BlockSpec((1, 8, LANES_BLK), lambda c, h: (top - c, 0, jnp.minimum(h, cap))),
        ],
        out_shape=[
            jax.ShapeDtypeStruct((seq_len, conv_dim), F32),
            jax.ShapeDtypeStruct((seq_len, n_blk * 128), F32),
            jax.ShapeDtypeStruct((seq_len, n_blk * 128), F32),
            jax.ShapeDtypeStruct((n_chunks, 8, d_inner), F32),
        ],
        scratch_shapes=[
            pltpu.VMEM((n_blk, STATE_DIM, LANES_BLK), F32),
            pltpu.VMEM((CHUNK_LEN, CHUNK_LEN), F32),
            pltpu.VMEM((CHUNK_LEN, CHUNK_LEN), F32),
            pltpu.VMEM((CHUNK_LEN, STATE_DIM), F32),
            pltpu.VMEM((CHUNK_LEN, STATE_DIM), F32),
        ],
        compiler_params=pltpu.CompilerParams(dimension_semantics=('arbitrary', 'arbitrary'), vmem_limit_bytes=40 * 2**20),
        cost_estimate=pl.CostEstimate(flops=150_000_000_000, bytes_accessed=100_000_000, transcendentals=0),
        name='ssd_backward',
    )(dy, y_all, xbc_act, xbc_act, xbc_act, dt_blk, cum_blk, cum_t, skip_row, prev_states)


def pre_norm(u_rows, norm_w):
    rows_f = u_rows.astype(F32)
    inv_rms = lax.rsqrt(jnp.mean(jnp.square(rows_f), axis=-1, keepdims=True) + NORM_EPS)
    return (rows_f * inv_rms * norm_w).astype(BF16)


def dt_part(dt_raw, dt_bias, a_log):
    dt_heads = jax.nn.softplus(dt_raw.astype(F32) + dt_bias)
    return dt_heads, dt_heads * -jnp.exp(a_log)


def delayed(vals, count, row):
    return vals if count == 0 else jnp.where(row >= count, pltpu.roll(vals, count, 0), 0.0)


def advanced(vals, count, row):
    seq_len = vals.shape[0]
    return vals if count == 0 else jnp.where(row < seq_len - count, pltpu.roll(vals, seq_len - count, 0), 0.0)


def conv_taps(p_ref, w_ref, bias_ref):
    x_cols = p_ref[...].astype(F32)
    row = lax.broadcasted_iota(jnp.int32, x_cols.shape, 0)
    n_taps = w_ref.shape[0]
    shifted = [delayed(x_cols, n_taps - 1 - tap, row) for tap in range(n_taps)]
    conv_out = bias_ref[...] + sum(shifted[tap] * w_ref[tap:tap + 1, :] for tap in range(n_taps))
    return row, shifted, conv_out


def conv_fwd_kernel(p_ref, w_ref, bias_ref, act_ref):
    _, _, conv_out = conv_taps(p_ref, w_ref, bias_ref)
    act_ref[...] = conv_out * jax.nn.sigmoid(conv_out)


def conv_bwd_kernel(p_ref, d_ref, w_ref, bias_ref, ddt_ref, dp_ref, gw_ref, *, n_cols):
    col = pl.program_id(0)

    @pl.when(col < n_cols)
    def _():
        row, shifted, conv_out = conv_taps(p_ref, w_ref, bias_ref)
        n_taps = len(shifted)
        sig = jax.nn.sigmoid(conv_out)
        d_conv = d_ref[...] * (sig * (1.0 + conv_out * (1.0 - sig)))
        d_p = sum(advanced(d_conv, n_taps - 1 - tap, row) * w_ref[tap:tap + 1, :] for tap in range(n_taps))
        dp_ref[...] = d_p.astype(BF16)
        rows = [jnp.sum(d_conv * part, axis=0, keepdims=True) for part in shifted]
        rows.append(jnp.sum(d_conv, axis=0, keepdims=True))
        rows.append(jnp.zeros((8 - len(rows), d_conv.shape[1]), F32))
        gw_ref[...] = jnp.concatenate(rows, axis=0)

    @pl.when(col == n_cols)
    def _():
        dp_ref[:, :128] = ddt_ref[...].astype(BF16)
        dp_ref[:, 128:] = jnp.zeros((dp_ref.shape[0], dp_ref.shape[1] - 128), BF16)


COLS_BLK = 256


def conv_forward(p_x, conv_w, conv_b):
    seq_len = p_x.shape[0]
    n_taps, conv_dim = conv_w.shape
    return pl.pallas_call(
        conv_fwd_kernel,
        grid=(conv_dim // COLS_BLK,),
        in_specs=[
            pl.BlockSpec((seq_len, COLS_BLK), lambda c: (0, c)),
            pl.BlockSpec((n_taps, COLS_BLK), lambda c: (0, c)),
            pl.BlockSpec((1, COLS_BLK), lambda c: (0, c)),
        ],
        out_specs=pl.BlockSpec((seq_len, COLS_BLK), lambda c: (0, c)),
        out_shape=jax.ShapeDtypeStruct((seq_len, conv_dim), F32),
        compiler_params=pltpu.CompilerParams(dimension_semantics=('arbitrary',), vmem_limit_bytes=40 * 2**20),
        cost_estimate=pl.CostEstimate(flops=20_000_000_000, bytes_accessed=33_000_000, transcendentals=0),
        name='conv_forward',
    )(p_x, conv_w, conv_b[None, :])


def conv_backward(p_x, d_act, conv_w, conv_b, d_dt_raw):
    seq_len, width = p_x.shape
    n_taps, conv_dim = conv_w.shape
    n_cols = conv_dim // COLS_BLK
    cap = n_cols - 1
    d_dt_raw = jnp.pad(d_dt_raw, ((0, 0), (0, 128 - d_dt_raw.shape[1])))
    return pl.pallas_call(
        functools.partial(conv_bwd_kernel, n_cols=n_cols),
        grid=(n_cols + 1,),
        in_specs=[
            pl.BlockSpec((seq_len, COLS_BLK), lambda c: (0, jnp.minimum(c, cap))),
            pl.BlockSpec((seq_len, COLS_BLK), lambda c: (0, jnp.minimum(c, cap))),
            pl.BlockSpec((n_taps, COLS_BLK), lambda c: (0, jnp.minimum(c, cap))),
            pl.BlockSpec((1, COLS_BLK), lambda c: (0, jnp.minimum(c, cap))),
            pl.BlockSpec((seq_len, 128), lambda c: (0, 0)),
        ],
        out_specs=[
            pl.BlockSpec((seq_len, COLS_BLK), lambda c: (0, c)),
            pl.BlockSpec((8, COLS_BLK), lambda c: (0, jnp.minimum(c, cap))),
        ],
        out_shape=[
            jax.ShapeDtypeStruct((seq_len, width), BF16),
            jax.ShapeDtypeStruct((8, conv_dim), F32),
        ],
        compiler_params=pltpu.CompilerParams(dimension_semantics=('arbitrary',), vmem_limit_bytes=40 * 2**20),
        cost_estimate=pl.CostEstimate(flops=50_000_000_000, bytes_accessed=44_000_000, transcendentals=0),
        name='conv_backward',
    )(p_x, d_act, conv_w, conv_b[None, :], d_dt_raw)


def gate_part(y_all, p_z, gate_w):
    gated_y = y_all * jax.nn.silu(p_z.astype(F32))
    normed = gated_y * lax.rsqrt(jnp.mean(jnp.square(gated_y), axis=-1, keepdims=True) + NORM_EPS)
    return (normed * gate_w).astype(BF16)


def layer_forward(u_rows, small, w_x, w_z, w_out):
    norm_w, conv_w, conv_b, dt_bias, a_log, d_skip, gate_w = small
    h_norm, norm_pull = jax.vjp(pre_norm, u_rows, norm_w)
    p_x = jnp.dot(h_norm, w_x, preferred_element_type=F32).astype(BF16)
    xbc_act = conv_forward(p_x, conv_w, conv_b)
    (dt_heads, a_heads), dt_pull = jax.vjp(dt_part, p_x[:, conv_w.shape[1]:].astype(F32), dt_bias, a_log)
    tables = head_tables(dt_heads, a_heads)
    skip_row = jnp.repeat(d_skip, HEAD_DIM)[None, :]
    y_all, prev_states = ssd_forward(xbc_act, *tables, skip_row)
    p_z = jnp.dot(h_norm, w_z, preferred_element_type=F32).astype(BF16)
    y_norm, gate_pull = jax.vjp(gate_part, y_all, p_z, gate_w)
    mixed = jnp.dot(y_norm, w_out, preferred_element_type=F32)
    out_rows = (u_rows.astype(F32) + mixed).astype(BF16)
    return out_rows, (h_norm, y_norm, norm_pull, p_x, dt_pull, gate_pull, xbc_act, tables, skip_row, y_all, prev_states)


def solution(mesh):
    dp_size = mesh.shape['dp']
    fsdp_size = mesh.shape['fsdp']
    act_spec = P(('dp', 'fsdp'), None, None)
    weight_specs = (P(None, 'fsdp'), P(None, 'fsdp', None), P(None, None, 'fsdp'), P(None, 'fsdp'), P(None, 'fsdp'), P(None, 'fsdp'), P(None, 'fsdp'), P(None, 'fsdp'), P(None, 'fsdp', None))
    swap = [(i, (i + 1) % dp_size) for i in range(dp_size)]

    def per_device(u_loc, g_loc, *pieces):
        batch_tot = u_loc.shape[0] * dp_size * fsdp_size
        small_ids = (0, 2, 3, 4, 5, 6, 7)
        d_inner = pieces[7].shape[1] * fsdp_size
        n_heads = pieces[4].shape[1] * fsdp_size

        packed = jnp.concatenate([pieces[i].astype(F32).reshape(-1) for i in small_ids])
        spread = lax.all_gather(packed, 'fsdp', axis=0, tiled=False)
        smalls = []
        offset = 0
        for i in small_ids:
            shape = pieces[i].shape
            count = pieces[i].size
            part = spread[:, offset:offset + count].reshape((fsdp_size,) + shape)
            part = jnp.moveaxis(part, 0, -2)
            smalls.append(part.reshape(shape[:-1] + (shape[-1] * fsdp_size,)))
            offset += count

        def gather(piece):
            return lax.all_gather(piece, 'fsdp', axis=0, tiled=True)

        w_full = []
        for layer in range(2):
            w_x = gather(pieces[1][layer, :, d_inner:])
            w_z = gather(pieces[1][layer, :, :d_inner])
            w_full.append((w_x, w_z, gather(pieces[8][layer])))

        def local_grad(lhs, rhs):
            grad = lax.dot_general(lhs, rhs, (((0,), (0,)), ((), ())), preferred_element_type=F32)
            return row_major((grad / batch_tot).astype(BF16))

        def scatter_sum(part_g):
            return lax.psum_scatter(part_g, 'fsdp', scatter_dimension=0, tiled=True)

        def dp_total(mine):
            total = mine.astype(F32)
            moving = mine
            for _ in range(dp_size - 1):
                moving = row_major(lax.ppermute(moving, 'dp', swap))
                total = total + moving.astype(F32)
            return row_major(total)

        def unpack(sums):
            return sums.reshape(sums.shape[0], -1, 128)[:, :, :HEADS_BLK].reshape(sums.shape[0], n_heads)

        def layer_backward(d_out, saved, weights, small, behind):
            h_norm, y_norm, norm_pull, p_x, dt_pull, gate_pull, xbc_act, tables, skip_row, y_all, prev_states = saved
            w_x, w_z, w_out = weights
            done = None
            g_out = local_grad(y_norm, d_out)
            d_out, g_out = lax.optimization_barrier((d_out, g_out))
            s_out = scatter_sum(g_out)
            d_ynorm = lax.dot_general(d_out, w_out, (((1,), (1,)), ((), ())), preferred_element_type=F32).astype(BF16)
            dy, d_pz, g_gate = gate_pull(d_ynorm)
            g_z = local_grad(h_norm, d_pz)
            if behind is not None:
                dy, g_z, s_z_old = lax.optimization_barrier((dy, g_z, behind[0]))
                t_z_old = dp_total(s_z_old)
            else:
                dy, g_z = lax.optimization_barrier((dy, g_z))
            s_z = row_major(scatter_sum(g_z).T)
            d_xbc, d_cum, d_dt, d_skip = ssd_backward(dy, y_all, xbc_act, *tables, skip_row, prev_states)
            if behind is not None:
                d_xbc, t_z_old, s_x_old, s_out = lax.optimization_barrier((d_xbc, t_z_old, behind[1], s_out))
                t_x_old = dp_total(s_x_old)
                t_out = dp_total(s_out)
            else:
                d_xbc, s_out = lax.optimization_barrier((d_xbc, s_out))
                t_out = dp_total(s_out)
            seq_len = dy.shape[0]
            n_chunks = seq_len // CHUNK_LEN
            upper = jnp.triu(jnp.ones((CHUNK_LEN, CHUNK_LEN), F32))
            d_a = jnp.einsum('qs,csh->cqh', upper, unpack(d_cum).reshape(n_chunks, CHUNK_LEN, n_heads), precision=lax.Precision.HIGHEST)
            d_dt_raw, g_dt_bias, g_a_log = dt_pull((unpack(d_dt), d_a.reshape(seq_len, n_heads)))
            d_px, g_conv = conv_backward(p_x, d_xbc, small[1], small[2], d_dt_raw)
            g_conv_w = g_conv[:small[1].shape[0]]
            g_conv_b = g_conv[small[1].shape[0]]
            g_x = local_grad(h_norm, d_px)
            if behind is not None:
                d_px, g_x, t_x_old, s_z = lax.optimization_barrier((d_px, g_x, t_x_old, s_z))
            else:
                d_px, g_x = lax.optimization_barrier((d_px, g_x))
            s_x = row_major(scatter_sum(g_x).T)
            d_h = lax.dot_general(d_pz, w_z, (((1,), (1,)), ((), ())), preferred_element_type=F32)
            d_h = (d_h + lax.dot_general(d_px, w_x, (((1,), (1,)), ((), ())), preferred_element_type=F32)).astype(BF16)
            d_u_norm, g_norm = norm_pull(d_h)
            d_u = (d_out.astype(F32) + d_u_norm.astype(F32)).astype(BF16)
            if behind is not None:
                done = (t_z_old, t_x_old)
            d_u, t_out = lax.optimization_barrier((d_u, t_out))
            g_skip = jnp.sum(jnp.sum(d_skip, axis=(0, 1)).reshape(n_heads, HEAD_DIM), axis=-1)
            small_g = (g_norm, g_conv_w, g_conv_b, g_dt_bias, g_a_log, g_skip, g_gate)
            return d_u, t_out, (s_z, s_x), done, small_g

        u_rows = u_loc[0]
        small_one = [s[0] for s in smalls]
        small_two = [s[1] for s in smalls]
        hidden, saved_one = layer_forward(u_rows, small_one, *w_full[0])
        out_rows, saved_two = layer_forward(hidden, small_two, *w_full[1])
        d_hidden, t_out_two, behind, _, sm_two = layer_backward(g_loc[0], saved_two, w_full[1], small_two, None)
        d_u, t_out_one, last, done_two, sm_one = layer_backward(d_hidden, saved_one, w_full[0], small_one, behind)
        t_z_one = dp_total(last[0])
        flat = []
        for one, two, i in zip(sm_one, sm_two, small_ids):
            for grad in (one, two):
                rounded = grad.astype(pieces[i].dtype) if pieces[i].dtype == BF16 else grad
                flat.append(rounded.astype(F32).reshape(-1))
        flat, t_z_one, s_x_one = lax.optimization_barrier((jnp.concatenate(flat), t_z_one, last[1]))
        t_x_one = dp_total(s_x_one)
        total = lax.psum(flat, ('dp', 'fsdp')) / batch_tot
        index = lax.axis_index('fsdp')
        small_out = []
        offset = 0
        for i, full in zip(small_ids, smalls):
            part = total[offset:offset + full.size].reshape(full.shape)
            offset += full.size
            width = pieces[i].shape[-1]
            small_out.append(lax.dynamic_slice_in_dim(part, index * width, width, axis=part.ndim - 1))
        g_in = jnp.zeros((pieces[1].shape[0], pieces[1].shape[2], pieces[1].shape[1]), F32)
        for layer, at_col, part in ((1, 0, done_two[0]), (1, d_inner, done_two[1]), (0, 0, t_z_one), (0, d_inner, t_x_one)):
            g_in = row_major(lax.dynamic_update_slice(g_in, part[None], (layer, at_col, 0)))
        g_in = jnp.swapaxes(g_in, 1, 2)
        g_w_out = jnp.zeros(pieces[8].shape, F32)
        for layer, part in ((1, t_out_two), (0, t_out_one)):
            g_w_out = lax.dynamic_update_slice(g_w_out, part[None], (layer, 0, 0))
        return (out_rows[None], d_u[None], small_out[0], g_in) + tuple(small_out[1:]) + (g_w_out,)

    return jax.shard_map(per_device, mesh=mesh, in_specs=(act_spec, act_spec) + weight_specs, out_specs=(act_spec, act_spec) + weight_specs, check_vma=False)
```
